32 devices in a mesh: ctx: 16 (over z, y, core), ch: 2 (over x).
Axes of the slice: x: 2, y: 2, z: 4, core: 2. Of those that a mesh axis runs over, the one named last changes fastest.
Arguments:
- tokens: bfloat16 [4096, 4096], P('ctx', 'ch'), may hold values from -6 to 6
- w_in: bfloat16 [4096, 3, 4096], P('ctx', None, 'ch'), may hold values from -0.09375 to 0.09375
- taps: float32 [3, 3, 4096], P(None, None, 'ch'), may hold values from -2 to 2
- modes_gain: float32 [16, 4096], P(None, 'ch'), may hold values from -1.5 to 1.5
- decay: float32 [16, 4096], P(None, 'ch'), may hold values from 0.3 to 300
- skip: float32 [4096], P('ch'), may hold values from -4 to 4
Outputs:
- mixed: bfloat16 [4096, 4096], P('ctx', 'ch')
The draws below stay inside these ranges and needn't reach their ends.
All inputs are finite; a program needn't handle non-finite values.
Results may differ from the reference program's by a relative error of at most 0.0075.
Values may be sent and summed in bfloat16 or wider, within the bound.
A program may use at most 128 MiB of HBM per device.

```python
import math
import jax
import jax.numpy as jnp

D = 4096
MODES = 16
SEQ = 4096


def level_of(key, extent, shards, smallest, high):
    level, own = 1.0, jax.random.fold_in(key, 6)
    for axis_at, parts in shards:
        heights = jnp.exp(jax.random.uniform(jax.random.fold_in(own, axis_at), (parts,), jnp.float32, smallest / len(shards), high / len(shards)))
        level = level * jnp.repeat(heights, extent[axis_at] // parts).reshape([-1 if axis == axis_at else 1 for axis in range(len(extent))])
    return level


def normal_values(rng, shape, scale, limit, pieces=(), kind=jnp.bfloat16):
    array = scale * jax.random.normal(rng, shape, jnp.float32)
    if pieces:
        array = array * level_of(rng, shape, pieces, -0.22, 0.18)
    return jnp.clip(array, -limit, limit).astype(kind)


def setup_inputs(seed: int = 0) -> dict:
    splits = jax.random.split(jax.random.key(seed), 7)
    return {
        "tokens": normal_values(splits[0], (SEQ, D), 1.0, 6.0, ((0, 16), (1, 2))),
        "w_in": normal_values(splits[1], (D, 3, D), D ** -0.5, 0.09375, ((0, 16), (2, 2))),
        "taps": normal_values(splits[2], (3, 3, D), 0.6, 2.0, ((2, 2),), jnp.float32),
        "modes_gain": normal_values(splits[3], (MODES, D), MODES ** -0.5, 1.5, ((1, 2),), jnp.float32),
        "decay": jnp.clip(jnp.exp(math.log(300.0) - 6.9077552 * jax.random.uniform(splits[4], (MODES, D), jnp.float32) ** level_of(splits[4], (MODES, D), ((1, 2),), -0.2, 0.2)), 0.3, 300.0),
        "skip": normal_values(splits[5], (D,), 1.0, 4.0, ((0, 2),), jnp.float32),
    }


def reference(tokens, w_in, taps, modes_gain, decay, skip):
    length, width = tokens.shape
    flat = w_in.reshape(width, 3 * width)
    projected = jnp.dot(tokens, flat, preferred_element_type=jnp.float32).astype(jnp.bfloat16)
    projected = projected.reshape(length, 3, width)
    extended = jnp.concatenate([jnp.zeros((2, 3, width), jnp.bfloat16), projected], 0).astype(jnp.float32)
    features = taps[0] * extended[2:] + taps[1] * extended[1:-1] + taps[2] * extended[:-2]
    gate_out = features[:, 0]
    product = features[:, 1] * features[:, 2]
    moments = jnp.arange(length, dtype=jnp.int32).astype(jnp.float32)[:, None]
    filt = jnp.zeros((length, width), jnp.float32)
    for index in range(decay.shape[0]):
        rate = decay[index] / length
        filt = filt + modes_gain[index] * jnp.sqrt(2.0 * rate) * jnp.exp(-rate * moments)
    total = 2 * length
    spectrum = jnp.fft.rfft(product, n=total, axis=0) * jnp.fft.rfft(filt, n=total, axis=0)
    conv = jnp.fft.irfft(spectrum, n=total, axis=0)[:length]
    return (gate_out * (conv + skip * product)).astype(jnp.bfloat16)
```

```python
import functools

import jax
import jax.numpy as jnp
from jax import lax
from jax.experimental import pallas as pl
from jax.experimental.pallas import tpu as pltpu
from jax.sharding import PartitionSpec as P

SEGS = 8
LANES = 128
MESH = pl.DeviceIdType.MESH


def flip(index, bits, count):
    out, bit = index, 1
    while bit < count:
        out = out + ((bits // bit) % 2) * (bit - 2 * bit * ((index // bit) % 2))
        bit *= 2
    return out


def piece_order(i, count):
    quarter = count // 4
    j = jnp.maximum(i - quarter, 0)
    later = quarter + quarter * (j % 3) + j // 3
    return jnp.where(i < quarter, i, later)


def kernel(
    n_ctx, n_ch, places,
    tokens, w_send, all_taps, all_gains, all_decay, all_skip, out,
    taps, gains, rates, skip, tok, w_recv, acc, prod, gate, state, ends, carry, sent, halo, halo_out,
    tok_ssem, tok_rsem, sib_ssem, w_ssem, w_rsem, f_ssem, f_rsem, out_ssem, out_rsem, st_ssem, st_rsem, halo_sems, local_sems, own_sems,
):
    rows, width = tokens.shape
    e_rows = w_send.shape[1]
    chips = n_ctx // 2
    teams = chips // places
    wide = w_send.shape[2] // places
    groups = wide // LANES
    lower = places // 2
    span = places * rows
    seg = span // SEGS
    header = SEGS
    modes = rates.shape[0]
    ctx, ch = lax.axis_index("ctx"), lax.axis_index("ch")
    chip, core = ctx // 2, ctx % 2
    team, place = chip // places, chip % places
    top, low = place // lower, place % lower
    other = 1 - core
    is_root = core == top
    sibling = (chip * 2 + other, ch)

    hops = [("low", b) for b in reversed([2**i for i in range(lower.bit_length() - 1)])]
    hops += [("ch", b) for b in reversed([2**i for i in range(n_ch.bit_length() - 1)])]
    depth = len(hops)

    def target(i):
        if i == depth:
            return (flip(chip, lower, chips) * 2 + core, ch)
        axis, bit = hops[i]
        return (flip(chip, bit, chips) * 2 + core, ch) if axis == "low" else (ctx, flip(ch, bit, n_ch))

    def slot_of(mask):
        lbits = sum(hops[i][1] for i in range(depth) if mask >> i & 1 and hops[i][0] == "low")
        hbits = sum(hops[i][1] for i in range(depth) if mask >> i & 1 and hops[i][0] == "ch")
        return flip(ch, hbits, n_ch) * lower + flip(low, lbits, lower)

    def unit(mask, c):
        return tok.at[slot_of(mask), pl.ds(pl.multiple_of(c * rows, 16), rows), :]

    barrier = pltpu.get_barrier_semaphore()

    @pl.loop(1, n_ctx)
    def _(m):
        pl.semaphore_signal(barrier, inc=1, device_id=(flip(ctx, m, n_ctx), ch), device_id_type=MESH)

    ch_hops = [i for i in range(depth) if hops[i][0] == "ch"]
    for i in ch_hops:
        pl.semaphore_signal(barrier, inc=1, device_id=target(i), device_id_type=MESH)

    own_tok = pltpu.make_async_copy(tokens, unit(0, core), local_sems.at[0])

    @pl.when(is_root)
    def _():
        own_tok.start()

    def w_columns(p, g):
        return w_send.at[:, :, pl.ds(pl.multiple_of(p * wide + g * LANES, LANES), LANES)]

    own_w = [pltpu.make_async_copy(w_columns(place, g), w_recv.at[g, 0, core], own_sems.at[0, g]) for g in range(groups)]
    for copy in own_w:
        copy.start()
    own_lanes = pl.ds(pl.multiple_of(place * wide, LANES), wide)
    own_small = [
        pltpu.make_async_copy(all_taps.at[:, :, own_lanes], taps, local_sems.at[1]),
        pltpu.make_async_copy(all_gains.at[:, own_lanes], gains, local_sems.at[2]),
        pltpu.make_async_copy(all_decay.at[:, own_lanes], rates, local_sems.at[3]),
        pltpu.make_async_copy(all_skip.at[:, own_lanes], skip, local_sems.at[4]),
    ]
    for copy in own_small:
        copy.start()
    pl.semaphore_wait(barrier, n_ctx - 1 + len(ch_hops))

    def tok_copy(mask, c, i, src=None):
        return pltpu.make_async_remote_copy(
            src_ref=unit(mask, c) if src is None else src,
            dst_ref=unit(mask, c),
            send_sem=tok_ssem.at[c, mask, i],
            recv_sem=tok_rsem.at[c, mask | (1 << i if i < depth else 0)],
            device_id=target(i),
            device_id_type=MESH,
        )

    sib_copy = pltpu.make_async_remote_copy(
        src_ref=tokens, dst_ref=unit(0, core), send_sem=sib_ssem, recv_sem=tok_rsem.at[core, 0], device_id=sibling, device_id_type=MESH
    )

    def tok_arrived(mask, c):
        pltpu.make_async_remote_copy(
            src_ref=unit(mask, c), dst_ref=unit(mask, c), send_sem=sib_ssem, recv_sem=tok_rsem.at[c, mask], device_id=sibling, device_id_type=MESH
        ).wait_recv()

    def relay(mask, c):
        for i in range(mask.bit_length(), depth):
            tok_copy(mask, c, i).start()

    def w_copy(m, g):
        peer = flip(chip, m, chips)
        return pltpu.make_async_remote_copy(
            src_ref=w_columns(peer % places, g),
            dst_ref=w_recv.at[g, m, core],
            send_sem=w_ssem.at[g, m],
            recv_sem=w_rsem.at[g, m],
            device_id=(peer * 2 + core, ch),
            device_id_type=MESH,
        )

    def f_copy(m, g, own=False):
        return pltpu.make_async_remote_copy(
            src_ref=w_columns(place, g) if own else w_recv.at[g, m, core],
            dst_ref=w_recv.at[g, m, core],
            send_sem=f_ssem.at[g, m],
            recv_sem=f_rsem.at[g, m],
            device_id=sibling,
            device_id_type=MESH,
        )

    def f_arrived(m, g):
        pltpu.make_async_remote_copy(
            src_ref=w_recv.at[g, m, other], dst_ref=w_recv.at[g, m, other], send_sem=f_ssem.at[g, m], recv_sem=f_rsem.at[g, m],
            device_id=sibling, device_id_type=MESH,
        ).wait_recv()

    @pl.when(is_root)
    def _():
        for i in [depth, *range(depth)]:
            tok_copy(0, core, i, tokens).start()

    @pl.when(jnp.logical_not(is_root))
    def _():
        sib_copy.start()

    f_copy(0, 0, True).start()

    @pl.when(is_root)
    def _():
        tok_arrived(0, other)
        for i in [depth, *range(depth)]:
            tok_copy(0, other, i).start()

    late = jnp.logical_and(core == 1, team < teams - 1) if groups > 1 and HOLD else None

    for g in range(groups):
        @pl.loop(1, chips)
        def _(i):
            m = piece_order(i, chips)
            if g > 0:
                skip_it = m == 1
                if g == groups - 1 and late is not None:
                    skip_it = jnp.logical_or(skip_it, jnp.logical_and(late, m >= places))

                @pl.when(jnp.logical_not(skip_it))
                def _():
                    w_copy(m, g).start()
            else:
                w_copy(m, g).start()

    acc[...] = jnp.zeros_like(acc)

    @pl.when(jnp.logical_not(is_root))
    def _():
        tok_arrived(0, core)
        relay(0, core)
        tok_arrived(0, other)
        relay(0, other)

    masks = sorted(range(1, 2**depth), key=lambda m: (m.bit_length(), bin(m).count("1"), m))
    n_low = lower.bit_length() - 1
    near = [mask for mask in masks if mask < 2**n_low]
    far = [mask for mask in masks if mask >= 2**n_low]

    def gather(which):
        for mask in which:
            for c in (core, other):
                tok_arrived(mask, c)
                relay(mask, c)

    gather(near)
    for g in range(1, groups):
        f_copy(0, g, True).start()
        w_copy(1, g).start()

    @pl.when(is_root)
    def _():
        own_tok.wait()
    for copy in own_small:
        copy.wait()
    rates[...] = rates[...] / (rows * n_ctx)

    per_half = chips // n_ch

    def near_first(i):
        return flip(ch, i // per_half, n_ch) * per_half + flip(chip % per_half, i % per_half, per_half)

    def in_order(i):
        return flip(chip, i, chips)

    def project(g, first, last, source):
        @pl.loop(first, last + 1)
        def _(i):
            @pl.when(i < last)
            def _():
                m = flip(chip, source(i), chips)

                @pl.when(m > 0)
                def _():
                    w_copy(m, g).wait_recv()
                    f_copy(m, g).start()

                @pl.when(m == 0)
                def _():
                    own_w[g].wait()

            @pl.when(i > first)
            def _():
                origin = source(i - 1)
                m = flip(chip, origin, chips)
                f_arrived(m, g)
                half, column = origin * 2 * e_rows // width, origin * 2 * e_rows % width
                left = tok[pl.ds(half * lower, lower), :, pl.ds(pl.multiple_of(column, LANES), 2 * e_rows)]
                left = left.reshape(span, 2 * e_rows)
                right = jnp.concatenate(
                    [jnp.concatenate([w_recv[g, m, c, j] for c in range(2)], axis=0) for j in range(3)], axis=1
                )
                acc[g, header:, :] += jnp.dot(left, right, preferred_element_type=jnp.float32)

    following = jnp.where(core == 0, sibling[0], (ctx + places * 2 - 1) % n_ctx)
    is_last = jnp.logical_and(core == 1, team == teams - 1)
    is_first = jnp.logical_and(core == 0, team == 0)

    def halo_copy(g):
        return pltpu.make_async_remote_copy(
            src_ref=halo_out.at[g],
            dst_ref=halo.at[g],
            send_sem=halo_sems.at[g, 0],
            recv_sem=halo_sems.at[g, 1],
            device_id=(following, ch),
            device_id_type=MESH,
        )

    def pair_copy(g):
        return pltpu.make_async_remote_copy(
            src_ref=ends.at[g, 0],
            dst_ref=carry.at[g, 0],
            send_sem=st_ssem.at[g, 0],
            recv_sem=st_rsem.at[g, 0],
            device_id=sibling,
            device_id_type=MESH,
        )

    def state_copy(g, k, c):
        return pltpu.make_async_remote_copy(
            src_ref=ends.at[g, 1],
            dst_ref=carry.at[g, k],
            send_sem=st_ssem.at[g, 2 * k - 1 + c],
            recv_sem=st_rsem.at[g, k],
            device_id=((chip + k * places) % chips * 2 + c, ch),
            device_id_type=MESH,
        )

    def row(ref, m, mine):
        return jnp.broadcast_to(ref[m : m + 1, mine], (SEGS, LANES))

    def lanes(g):
        return slice(g * LANES, (g + 1) * LANES)

    def first_half(g):
        mine = lanes(g)
        halo_out[g] = acc[g, span : span + header, :]

        @pl.when(jnp.logical_not(is_last))
        def _():
            halo_copy(g).start()

        @pl.when(is_first)
        def _():
            acc[g, 0:header, :] = jnp.zeros((header, acc.shape[2]), jnp.float32)

        @pl.when(jnp.logical_not(is_first))
        def _():
            halo_copy(g).wait_recv()
            acc[g, 0:header, :] = halo[g]

        @pl.loop(0, SEGS)
        def _(s):
            base = pl.multiple_of(s * seg, 8)
            features = []
            for j in range(3):
                block = acc[g, pl.ds(base, seg + header), j * LANES : (j + 1) * LANES]
                block = block.astype(jnp.bfloat16).astype(jnp.float32)
                total = taps[0, j : j + 1, mine] * block[header:]
                total += taps[1, j : j + 1, mine] * pltpu.roll(block, 1, 0)[header:]
                total += taps[2, j : j + 1, mine] * pltpu.roll(block, 2, 0)[header:]
                features.append(total)
            gate[g, pl.ds(s, seg, stride=SEGS), :] = features[0]
            prod[g, pl.ds(s, seg, stride=SEGS), :] = features[1] * features[2]

        keep = [jnp.exp(-row(rates, m, mine)) for m in range(modes)]

        def first_step(t, states):
            x = prod[g, pl.ds(pl.multiple_of(t * SEGS, SEGS), SEGS), :]
            return tuple(a * s + x for a, s in zip(keep, states))

        zeros = tuple(jnp.zeros((SEGS, LANES), jnp.float32) for _ in range(modes))
        last = lax.fori_loop(0, seg, first_step, zeros, unroll=2)
        for m in range(modes):
            state[g, m] = last[m]

        rate = rates[:, mine]
        jump = jnp.exp(-rate * float(seg))
        running = jnp.zeros_like(jump)
        for s in range(SEGS):
            ending = state[g, :, s, :]
            state[g, :, s, :] = running
            running = running * jump + ending
        ends[g, 0] = running

        @pl.when(core == 0)
        def _():
            pair_copy(g).start()

        @pl.when(core == 1)
        def _():
            pair_copy(g).wait_recv()
            ends[g, 1] = ends[g, 0] + carry[g, 0] * jnp.exp(-rate * float(span))
            for k in range(1, teams):
                @pl.when(team + k < teams)
                def _():
                    for c in range(2):
                        state_copy(g, k, c).start()

    def second_half(g):
        mine = lanes(g)
        rate = rates[:, mine]
        incoming = jnp.zeros_like(rate)
        ends[g, 2] = incoming
        for k in range(1, teams):
            @pl.when(team >= k)
            def _():
                state_copy(g, k, core).wait_recv()
                ends[g, 2] += carry[g, k] * jnp.exp(-rate * float((k - 1) * 2 * span))

        @pl.when(core == 1)
        def _():
            ends[g, 2] = ends[g, 2] * jnp.exp(-rate * float(span)) + carry[g, 0]

        incoming = ends[g, 2]
        for s in range(SEGS):
            state[g, :, s, :] = state[g, :, s, :] + incoming * jnp.exp(-rate * float(s * seg))

        keep = [jnp.exp(-row(rates, m, mine)) for m in range(modes)]
        weight = [row(gains, m, mine) * jnp.sqrt(2.0 * row(rates, m, mine)) for m in range(modes)]
        direct = jnp.broadcast_to(skip[0:1, mine], (SEGS, LANES))

        def second_step(t, states):
            where = pl.ds(pl.multiple_of(t * SEGS, SEGS), SEGS)
            x = prod[g, where, :]
            states = tuple(a * s + x for a, s in zip(keep, states))
            terms = [w * s for w, s in zip(weight, states)] + [direct * x]
            while len(terms) > 1:
                terms = [a + b for a, b in zip(terms[::2], terms[1::2])] + ([terms[-1]] if len(terms) % 2 else [])
            gate[g, where, :] = gate[g, where, :] * terms[0]
            return states

        lax.fori_loop(0, seg, second_step, tuple(state[g, m] for m in range(modes)))

        @pl.loop(0, SEGS)
        def _(s):
            value = gate[g, pl.ds(s, seg, stride=SEGS), :]
            sent[g, pl.ds(pl.multiple_of(s * seg, 8), seg), :] = value.astype(sent.dtype)

        @pl.when(is_root)
        def _():
            own_out(g).start()

        @pl.when(jnp.logical_not(is_root))
        def _():
            out_copy(0, g).start()

        @pl.loop(1, places)
        def _(d):
            out_copy(places - d, g).start()

    def columns(p, g):
        return out.at[:, pl.ds(pl.multiple_of(p * wide + g * LANES, LANES), LANES)]

    def out_rows(d, g):
        return sent.at[g, pl.ds(pl.multiple_of(d * rows, 16), rows), :]

    def own_out(g):
        return pltpu.make_async_copy(out_rows(low * 2 + core, g), columns(place, g), own_sems.at[1, g])

    def out_copy(o, g):
        d = flip(low * 2 + core, o, places)
        peer = team * places + core * lower + d // 2
        return pltpu.make_async_remote_copy(
            src_ref=out_rows(d, g),
            dst_ref=columns(place, g),
            send_sem=out_ssem.at[g, o],
            recv_sem=out_rsem.at[g, place],
            device_id=(peer * 2 + d % 2, ch),
            device_id_type=MESH,
        )

    def out_arrived(p, g):
        pltpu.make_async_remote_copy(
            src_ref=columns(p, g), dst_ref=columns(p, g), send_sem=out_ssem.at[g, 0], recv_sem=out_rsem.at[g, p],
            device_id=sibling, device_id_type=MESH,
        ).wait_recv()

    for g in range(groups - 1):
        project(g, 0, per_half, near_first)
    gather(far)
    for g in range(groups - 1):
        project(g, per_half, chips, near_first)
        first_half(g)
        if g > 0:
            second_half(g - 1)
    if groups > 1:
        if late is not None:
            @pl.when(late)
            def _():
                @pl.loop(places, chips)
                def _(i):
                    w_copy(i, groups - 1).start()

        project(groups - 1, 0, places, in_order)
        second_half(groups - 2)
        project(groups - 1, places, chips, in_order)
    else:
        project(0, 0, chips, in_order)
    first_half(groups - 1)
    second_half(groups - 1)

    @pl.when(is_root)
    def _():
        for c in (core, other):
            for i in range(depth + 1):
                tok_copy(0, c, i).wait_send()

    @pl.when(jnp.logical_not(is_root))
    def _():
        sib_copy.wait_send()
        for c in (core, other):
            for i in range(depth):
                tok_copy(0, c, i).wait_send()

    for mask in masks:
        for c in (core, other):
            for i in range(mask.bit_length(), depth):
                tok_copy(mask, c, i).wait_send()

    for g in range(groups):
        f_copy(0, g, True).wait_send()

        @pl.loop(1, chips)
        def _(m):
            w_copy(m, g).wait_send()
            f_copy(m, g).wait_send()

        @pl.when(jnp.logical_not(is_last))
        def _():
            halo_copy(g).wait_send()

        @pl.when(core == 0)
        def _():
            pair_copy(g).wait_send()

        for k in range(1, teams):
            @pl.when(jnp.logical_and(core == 1, team + k < teams))
            def _():
                for c in range(2):
                    state_copy(g, k, c).wait_send()

        @pl.when(is_root)
        def _():
            own_out(g).wait()

        @pl.when(jnp.logical_not(is_root))
        def _():
            out_copy(0, g).wait_send()

        @pl.loop(1, places)
        def _(d):
            out_copy(d, g).wait_send()

        @pl.loop(0, places)
        def _(p):
            @pl.when(jnp.logical_or(p != place, jnp.logical_not(is_root)))
            def _():
                out_arrived(p, g)


HOLD = True


def body(n_ctx, n_ch, tokens, w_in, taps, modes_gain, decay, skip):
    rows, width = tokens.shape
    e_rows, _, channels = w_in.shape
    modes = decay.shape[0]
    chips = n_ctx // 2
    places = min(chips // 2, channels // LANES)
    teams = chips // places
    wide = channels // places
    span = places * rows
    groups = wide // LANES
    lower = places // 2
    depth = (lower * n_ch).bit_length() - 1
    w_send = w_in.transpose(1, 0, 2)
    hbm = pl.BlockSpec(memory_space=pl.ANY)
    dma = pltpu.SemaphoreType.DMA
    f32 = jnp.float32
    return pl.pallas_call(
        functools.partial(kernel, n_ctx, n_ch, places),
        out_shape=jax.ShapeDtypeStruct((rows, channels), jnp.bfloat16),
        in_specs=[hbm] * 6,
        out_specs=hbm,
        scratch_shapes=[
            pltpu.VMEM((3, 3, wide), f32),
            pltpu.VMEM((modes, wide), f32),
            pltpu.VMEM((modes, wide), f32),
            pltpu.VMEM((1, wide), f32),
            pltpu.VMEM((n_ch * lower, 2 * rows, width), tokens.dtype),
            pltpu.VMEM((groups, chips, 2, 3, e_rows, LANES), w_in.dtype),
            pltpu.VMEM((groups, SEGS + span, 3 * LANES), f32),
            pltpu.VMEM((groups, span, LANES), f32),
            pltpu.VMEM((groups, span, LANES), f32),
            pltpu.VMEM((groups, modes, SEGS, LANES), f32),
            pltpu.VMEM((groups, 3, modes, LANES), f32),
            pltpu.VMEM((groups, teams, modes, LANES), f32),
            pltpu.VMEM((groups, span, LANES), jnp.bfloat16),
            pltpu.VMEM((groups, SEGS, 3 * LANES), f32),
            pltpu.VMEM((groups, SEGS, 3 * LANES), f32),
            dma((2, 2**depth, depth + 1)),
            dma((2, 2**depth)),
            dma,
            dma((groups, chips)),
            dma((groups, chips)),
            dma((groups, chips)),
            dma((groups, chips)),
            dma((groups, places)),
            dma((groups, places)),
            dma((groups, 2 * teams)),
            dma((groups, teams)),
            dma((groups, 2)),
            dma((5,)),
            dma((2, groups)),
        ],
        compiler_params=pltpu.CompilerParams(
            collective_id=0, has_side_effects=True, vmem_limit_bytes=48 * 1024 * 1024
        ),
    )(tokens, w_send, taps, modes_gain, decay, skip[None])


def solution(mesh):
    in_specs = (
        P("ctx", "ch"),
        P("ctx", None, "ch"),
        P(None, None, "ch"),
        P(None, "ch"),
        P(None, "ch"),
        P("ch"),
    )
    step = functools.partial(body, mesh.shape["ctx"], mesh.shape["ch"])
    return jax.shard_map(step, mesh=mesh, in_specs=in_specs, out_specs=P("ctx", "ch"), check_vma=False)
```

```python
import functools

import jax
import jax.numpy as jnp
from jax import lax
from jax.experimental import pallas as pl
from jax.experimental.pallas import tpu as pltpu
from jax.sharding import PartitionSpec as P

SEGS = 8
LANES = 128
HELD = 2


def flip(index, bits):
    out, bit = index, 1
    while bit <= bits:
        if bits & bit:
            out = out + bit - 2 * bit * ((index // bit) % 2)
        bit *= 2
    return out


def flip_traced(index, bits, count):
    out, bit = index, 1
    while bit < count:
        out = out + ((bits // bit) % 2) * (bit - 2 * bit * ((index // bit) % 2))
        bit *= 2
    return out


def piece_order(i, count):
    quarter = count // 4
    j = jnp.maximum(i - quarter, 0)
    turn = j % 3
    later = quarter + quarter * turn + j // 3
    return jnp.where(i < quarter, i, later)


def kernel(
    n_ctx, n_ch, groups,
    tokens, w_send, all_taps, all_gains, all_decay, all_skip, out,
    taps, gains, rates, skip, tok, w_recv, acc, prod, gate, state, ends, carry, sent, halo, halo_out,
    tok_ssem, tok_rsem, w_ssem, w_rsem, out_ssem, out_rsem, st_ssem, st_rsem, halo_sems, local_sems, own_sems,
):
    rows, width = tokens.shape
    wide = w_send.shape[2] // groups
    teams = n_ctx // groups
    span = groups * rows
    seg = span // SEGS
    lane_groups = wide // LANES
    ctx, ch = lax.axis_index("ctx"), lax.axis_index("ch")
    team, place = ctx // groups, ctx % groups

    hops = [("ctx", b) for b in reversed([2**i for i in range(1, groups.bit_length() - 1)])]
    hops += [("ch", b) for b in reversed([2**i for i in range(n_ch.bit_length() - 1)])]
    hops += [("ctx", 1)]
    depth = len(hops)

    def target(hop):
        axis, bit = hop
        return (flip(ctx, bit), ch) if axis == "ctx" else (ctx, flip(ch, bit))

    def slot_of(mask):
        cbits = sum(hops[i][1] for i in range(depth) if mask >> i & 1 and hops[i][0] == "ctx")
        hbits = sum(hops[i][1] for i in range(depth) if mask >> i & 1 and hops[i][0] == "ch")
        return flip(ch, hbits) * groups + flip(place, cbits)

    barrier = pltpu.get_barrier_semaphore()

    @pl.loop(1, n_ctx)
    def _(m):
        pl.semaphore_signal(barrier, inc=1, device_id=(flip_traced(ctx, m, n_ctx), ch), device_id_type=pl.DeviceIdType.MESH)

    ch_hops = [hop for hop in hops if hop[0] == "ch"]
    for hop in ch_hops:
        pl.semaphore_signal(barrier, inc=1, device_id=target(hop), device_id_type=pl.DeviceIdType.MESH)
    own_tok = pltpu.make_async_copy(tokens, tok.at[slot_of(0)], local_sems.at[0])
    own_tok.start()

    def w_columns(p, g):
        return w_send.at[:, :, pl.ds(pl.multiple_of(p * wide + g * LANES, LANES), LANES)]

    own_w = [pltpu.make_async_copy(w_columns(place, g), w_recv.at[g, 0], own_sems.at[0, g]) for g in range(lane_groups)]
    for copy in own_w:
        copy.start()
    own_lanes = pl.ds(pl.multiple_of(place * wide, LANES), wide)
    own_small = [
        pltpu.make_async_copy(all_taps.at[:, :, own_lanes], taps, local_sems.at[3]),
        pltpu.make_async_copy(all_gains.at[:, own_lanes], gains, local_sems.at[4]),
        pltpu.make_async_copy(all_decay.at[:, own_lanes], rates, local_sems.at[5]),
        pltpu.make_async_copy(all_skip.at[:, own_lanes], skip, local_sems.at[6]),
    ]
    for copy in own_small:
        copy.start()
    pl.semaphore_wait(barrier, n_ctx - 1 + len(ch_hops))

    def tok_copy(mask, i):
        src = tokens if mask == 0 else tok.at[slot_of(mask)]
        return pltpu.make_async_remote_copy(
            src_ref=src,
            dst_ref=tok.at[slot_of(mask)],
            send_sem=tok_ssem.at[mask, i],
            recv_sem=tok_rsem.at[mask | 1 << i],
            device_id=target(hops[i]),
            device_id_type=pl.DeviceIdType.MESH,
        )

    def arrived(mask):
        top = mask.bit_length() - 1
        pltpu.make_async_remote_copy(
            src_ref=tok.at[slot_of(mask)],
            dst_ref=tok.at[slot_of(mask)],
            send_sem=tok_ssem.at[0, top],
            recv_sem=tok_rsem.at[mask],
            device_id=target(hops[top]),
            device_id_type=pl.DeviceIdType.MESH,
        ).wait_recv()

    for i in range(depth):
        tok_copy(0, i).start()

    def w_copy(m, g):
        peer = flip_traced(ctx, m, n_ctx)
        return pltpu.make_async_remote_copy(
            src_ref=w_columns(peer % groups, g),
            dst_ref=w_recv.at[g, m],
            send_sem=w_ssem.at[g, m],
            recv_sem=w_rsem.at[g, m],
            device_id=(peer, ch),
            device_id_type=pl.DeviceIdType.MESH,
        )

    waiting = team < teams - 1

    def send(g, first, last):
        @pl.loop(first, last)
        def _(i):
            w_copy(2 * piece_order(i // 2, n_ctx // 2) + i % 2, g).start()

    for g in range(lane_groups - 1):
        send(g, 1, n_ctx)
    if lane_groups > 1:
        send(lane_groups - 1, 1, n_ctx - HELD)

        @pl.when(jnp.logical_not(waiting))
        def _():
            send(lane_groups - 1, n_ctx - HELD, n_ctx)
    else:
        send(0, 1, n_ctx)

    acc[...] = jnp.zeros_like(acc)
    masks = sorted(range(1, 2**depth), key=lambda m: (m.bit_length() if m.bit_length() == depth else 0, bin(m).count("1"), m))
    crossing = sum(1 << i for i in range(depth) if hops[i][0] == "ch")

    def gather(which):
        for mask in which:
            arrived(mask)
            for i in range(mask.bit_length(), depth):
                tok_copy(mask, i).start()

    gather([mask for mask in masks if not mask & crossing])
    own_tok.wait()
    for copy in own_w + own_small:
        copy.wait()
    rates[...] = rates[...] / (rows * n_ctx)

    header = SEGS

    modes = rates.shape[0]
    depth_rows = w_recv.shape[3]
    columns = [pl.ds(pl.multiple_of(place * wide + g * LANES, LANES), LANES) for g in range(lane_groups)]

    chips = n_ctx // 2
    per_half = chips // n_ch

    def near_first(i):
        home = ctx // 2
        origin = flip_traced(ch, i // per_half, n_ch) * per_half + flip_traced(home % per_half, i % per_half, per_half)
        return flip_traced(home, origin, chips)

    def in_order(i):
        return piece_order(i, chips)

    def project(g, first, last, source):
        @pl.loop(first, last)
        def _(i):
            m = 2 * source(i)
            odd = ctx % 2

            @pl.when(m > 0)
            def _():
                w_copy(m, g).wait_recv()

            w_copy(m + 1, g).wait_recv()
            origin = flip_traced(ctx - odd, m, n_ctx) * depth_rows
            half, column = origin // width, origin % width
            left = tok[pl.ds(half * groups, groups), :, pl.ds(pl.multiple_of(column, LANES), 2 * depth_rows)]
            left = left.reshape(span, 2 * depth_rows)
            pair = (m + odd, m + 1 - odd)
            right = jnp.concatenate(
                [jnp.concatenate([w_recv[g, p, j] for p in pair], axis=0) for j in range(3)], axis=1
            )
            acc[g, header:, :] += jnp.dot(left, right, preferred_element_type=jnp.float32)

    def halo_copy(g):
        return pltpu.make_async_remote_copy(
            src_ref=halo_out.at[g],
            dst_ref=halo.at[g],
            send_sem=halo_sems.at[g, 0],
            recv_sem=halo_sems.at[g, 1],
            device_id=((ctx + groups) % n_ctx, ch),
            device_id_type=pl.DeviceIdType.MESH,
        )

    def state_copy(k, g):
        return pltpu.make_async_remote_copy(
            src_ref=ends.at[g],
            dst_ref=carry.at[g, k],
            send_sem=st_ssem.at[g, k],
            recv_sem=st_rsem.at[g, k],
            device_id=((ctx + k * groups) % n_ctx, ch),
            device_id_type=pl.DeviceIdType.MESH,
        )

    def send_halo(g):
        halo_out[g] = acc[g, span : span + header, :]

        @pl.when(team < teams - 1)
        def _():
            halo_copy(g).start()

    def row(ref, m, mine):
        return jnp.broadcast_to(ref[m : m + 1, mine], (SEGS, LANES))

    def decays(mine):
        return [jnp.exp(-row(rates, m, mine)) for m in range(modes)]

    def first_half(g):
        mine = slice(g * LANES, (g + 1) * LANES)

        @pl.loop(1, SEGS + 1)
        def _(turn):
            s = turn % SEGS

            @pl.when(s == 0)
            def _():
                @pl.when(team == 0)
                def _():
                    acc[g, 0:header, :] = jnp.zeros((header, acc.shape[2]), jnp.float32)

                @pl.when(team > 0)
                def _():
                    halo_copy(g).wait_recv()
                    acc[g, 0:header, :] = halo[g]

            base = pl.multiple_of(s * seg, 8)
            features = []
            for j in range(3):
                block = acc[g, pl.ds(base, seg + header), j * LANES : (j + 1) * LANES]
                block = block.astype(jnp.bfloat16).astype(jnp.float32)
                total = taps[0, j : j + 1, mine] * block[header:]
                total += taps[1, j : j + 1, mine] * pltpu.roll(block, 1, 0)[header:]
                total += taps[2, j : j + 1, mine] * pltpu.roll(block, 2, 0)[header:]
                features.append(total)
            gate[g, pl.ds(s, seg, stride=SEGS), :] = features[0]
            prod[g, pl.ds(s, seg, stride=SEGS), :] = features[1] * features[2]

        keep = decays(mine)

        def first_step(t, states):
            x = prod[g, pl.ds(pl.multiple_of(t * SEGS, SEGS), SEGS), :]
            return tuple(a * s + x for a, s in zip(keep, states))

        zeros = tuple(jnp.zeros((SEGS, LANES), jnp.float32) for _ in range(modes))
        last = lax.fori_loop(0, seg, first_step, zeros, unroll=4)
        for m in range(modes):
            state[g, m] = last[m]

        rate = rates[:, mine]
        jump = jnp.exp(-rate * float(seg))
        running = jnp.zeros_like(jump)
        for s in range(SEGS):
            ending = state[g, :, s, :]
            state[g, :, s, :] = running
            running = running * jump + ending
        ends[g] = running
        carry[g, 0] = jnp.zeros_like(jump)
        for k in range(1, teams):
            @pl.when(team + k < teams)
            def _():
                state_copy(k, g).start()

    def second_half(g):
        mine = slice(g * LANES, (g + 1) * LANES)
        rate = rates[:, mine]
        for k in range(1, teams):
            @pl.when(team >= k)
            def _():
                state_copy(k, g).wait_recv()
                carry[g, 0] += carry[g, k] * jnp.exp(-rates[:, mine] * float((k - 1) * span))
        incoming = carry[g, 0]
        for s in range(SEGS):
            state[g, :, s, :] = state[g, :, s, :] + incoming * jnp.exp(-rate * float(s * seg))

        keep = decays(mine)
        weight = [row(gains, m, mine) * jnp.sqrt(2.0 * row(rates, m, mine)) for m in range(modes)]
        direct = jnp.broadcast_to(skip[0:1, mine], (SEGS, LANES))

        def second_step(t, states):
            where = pl.ds(pl.multiple_of(t * SEGS, SEGS), SEGS)
            x = prod[g, where, :]
            states = tuple(a * s + x for a, s in zip(keep, states))
            terms = [w * s for w, s in zip(weight, states)] + [direct * x]
            while len(terms) > 1:
                terms = [a + b for a, b in zip(terms[::2], terms[1::2])] + ([terms[-1]] if len(terms) % 2 else [])
            gate[g, where, :] = gate[g, where, :] * terms[0]
            return states

        lax.fori_loop(0, seg, second_step, tuple(state[g, m] for m in range(modes)), unroll=4)

        @pl.loop(0, SEGS)
        def _(s):
            value = gate[g, pl.ds(s, seg, stride=SEGS), :]
            sent[g, pl.ds(pl.multiple_of(s * seg, 8), seg), :] = value.astype(sent.dtype)

    def out_rows(p, g):
        return sent.at[g, pl.ds(pl.multiple_of(p * rows, 16), rows), :]

    def out_copy(d, g):
        peer = flip_traced(place, d, groups)
        return pltpu.make_async_remote_copy(
            src_ref=out_rows(peer, g),
            dst_ref=out.at[:, columns[g]],
            send_sem=out_ssem.at[g, d],
            recv_sem=out_rsem.at[g, d],
            device_id=(team * groups + peer, ch),
            device_id_type=pl.DeviceIdType.MESH,
        )

    def out_arrival(d, g):
        peer = flip_traced(place, d, groups)
        spot = out.at[:, pl.ds(pl.multiple_of(peer * wide + g * LANES, LANES), LANES)]
        return pltpu.make_async_remote_copy(
            src_ref=spot,
            dst_ref=spot,
            send_sem=out_ssem.at[g, d],
            recv_sem=out_rsem.at[g, d],
            device_id=(team * groups + peer, ch),
            device_id_type=pl.DeviceIdType.MESH,
        )

    own_out = [pltpu.make_async_copy(out_rows(place, g), out.at[:, columns[g]], own_sems.at[1, g]) for g in range(lane_groups)]
    def give_out(g):
        @pl.loop(1, groups)
        def _(d):
            out_copy(groups - d, g).start()

        own_out[g].start()

    tail = lane_groups - 1
    far = [mask for mask in masks if mask & crossing]
    if tail:
        project(0, 0, per_half, near_first)
    gather(far)
    for g in range(tail):
        project(g, per_half if g == 0 else 0, chips, near_first)
        send_halo(g)
        first_half(g)
        if g == tail - 1:
            @pl.when(waiting)
            def _():
                send(tail, n_ctx - HELD, n_ctx)

        if g < tail - 1:
            second_half(g)
            give_out(g)
    half_way = chips // 2
    if tail:
        project(tail, 0, half_way, in_order)
        second_half(tail - 1)
        give_out(tail - 1)
        project(tail, half_way, chips, in_order)
    else:
        project(0, 0, chips, in_order)
    send_halo(tail)
    first_half(tail)
    second_half(tail)
    give_out(tail)

    for i in range(depth):
        tok_copy(0, i).wait_send()
    for mask in masks:
        for i in range(mask.bit_length(), depth):
            tok_copy(mask, i).wait_send()

    for g in range(lane_groups):
        @pl.loop(1, n_ctx)
        def _(m):
            w_copy(m, g).wait_send()

        @pl.when(team < teams - 1)
        def _():
            halo_copy(g).wait_send()

        for k in range(1, teams):
            @pl.when(team + k < teams)
            def _():
                state_copy(k, g).wait_send()

        @pl.loop(1, groups)
        def _(d):
            out_arrival(d, g).wait_recv()
            out_copy(d, g).wait_send()

        own_out[g].wait()


def body(n_ctx, n_ch, tokens, w_in, taps, modes_gain, decay, skip):
    rows, width = tokens.shape
    e_rows, _, channels = w_in.shape
    modes = decay.shape[0]
    groups = min(n_ctx // 2, channels // LANES)
    teams = n_ctx // groups
    wide = channels // groups
    span = groups * rows
    parts = wide // LANES
    depth = (groups * n_ch).bit_length() - 1
    w_send = w_in.transpose(1, 0, 2)
    hbm = pl.BlockSpec(memory_space=pl.ANY)
    dma = pltpu.SemaphoreType.DMA
    f32 = jnp.float32
    return pl.pallas_call(
        functools.partial(kernel, n_ctx, n_ch, groups),
        out_shape=jax.ShapeDtypeStruct((rows, channels), jnp.bfloat16),
        in_specs=[hbm] * 6,
        out_specs=hbm,
        scratch_shapes=[
            pltpu.VMEM((3, 3, wide), f32),
            pltpu.VMEM((modes, wide), f32),
            pltpu.VMEM((modes, wide), f32),
            pltpu.VMEM((1, wide), f32),
            pltpu.VMEM((n_ch * groups, rows, width), tokens.dtype),
            pltpu.VMEM((parts, n_ctx, 3, e_rows, LANES), w_in.dtype),
            pltpu.VMEM((parts, SEGS + span, 3 * LANES), f32),
            pltpu.VMEM((parts, span, LANES), f32),
            pltpu.VMEM((parts, span, LANES), f32),
            pltpu.VMEM((parts, modes, SEGS, LANES), f32),
            pltpu.VMEM((parts, modes, LANES), f32),
            pltpu.VMEM((parts, teams, modes, LANES), f32),
            pltpu.VMEM((parts, span, LANES), jnp.bfloat16),
            pltpu.VMEM((parts, SEGS, 3 * LANES), f32),
            pltpu.VMEM((parts, SEGS, 3 * LANES), f32),
            dma((2**depth, depth)),
            dma((2**depth,)),
            dma((parts, n_ctx)),
            dma((parts, n_ctx)),
            dma((parts, groups)),
            dma((parts, groups)),
            dma((parts, teams)),
            dma((parts, teams)),
            dma((parts, 2)),
            dma((7,)),
            dma((2, parts)),
        ],
        compiler_params=pltpu.CompilerParams(
            collective_id=0, has_side_effects=True, vmem_limit_bytes=60 * 1024 * 1024
        ),
    )(tokens, w_send, taps, modes_gain, decay, skip[None])


def solution(mesh):
    in_specs = (
        P("ctx", "ch"),
        P("ctx", None, "ch"),
        P(None, None, "ch"),
        P(None, "ch"),
        P(None, "ch"),
        P("ch"),
    )
    step = functools.partial(body, mesh.shape["ctx"], mesh.shape["ch"])
    return jax.shard_map(step, mesh=mesh, in_specs=in_specs, out_specs=P("ctx", "ch"), check_vma=False)
```

```python
import functools

import jax
import jax.numpy as jnp
from jax import lax
from jax.experimental import pallas as pl
from jax.experimental.pallas import tpu as pltpu
from jax.sharding import PartitionSpec as P

SEGS = 8
LANES = 128
HELD = 2


def flip(index, bits):
    out, bit = index, 1
    while bit <= bits:
        if bits & bit:
            out = out + bit - 2 * bit * ((index // bit) % 2)
        bit *= 2
    return out


def flip_traced(index, bits, count):
    out, bit = index, 1
    while bit < count:
        out = out + ((bits // bit) % 2) * (bit - 2 * bit * ((index // bit) % 2))
        bit *= 2
    return out


def piece_order(i, count):
    quarter = count // 4
    j = jnp.maximum(i - quarter, 0)
    turn = j % 3
    later = quarter + quarter * turn + j // 3
    return jnp.where(i < quarter, i, later)


def kernel(
    n_ctx, n_ch, groups,
    tokens, w_send, all_taps, all_gains, all_decay, all_skip, out,
    taps, gains, rates, skip, tok, w_recv, acc, prod, gate, state, ends, carry, sent, halo, halo_out,
    tok_ssem, tok_rsem, w_ssem, w_rsem, out_ssem, out_rsem, st_ssem, st_rsem, halo_sems, local_sems, own_sems,
):
    rows, width = tokens.shape
    wide = w_send.shape[2] // groups
    teams = n_ctx // groups
    span = groups * rows
    seg = span // SEGS
    lane_groups = wide // LANES
    ctx, ch = lax.axis_index("ctx"), lax.axis_index("ch")
    team, place = ctx // groups, ctx % groups

    hops = [("ctx", b) for b in reversed([2**i for i in range(1, groups.bit_length() - 1)])]
    hops += [("ch", b) for b in reversed([2**i for i in range(n_ch.bit_length() - 1)])]
    hops += [("ctx", 1)]
    depth = len(hops)

    def target(hop):
        axis, bit = hop
        return (flip(ctx, bit), ch) if axis == "ctx" else (ctx, flip(ch, bit))

    def slot_of(mask):
        cbits = sum(hops[i][1] for i in range(depth) if mask >> i & 1 and hops[i][0] == "ctx")
        hbits = sum(hops[i][1] for i in range(depth) if mask >> i & 1 and hops[i][0] == "ch")
        return flip(ch, hbits) * groups + flip(place, cbits)

    barrier = pltpu.get_barrier_semaphore()

    @pl.loop(1, n_ctx)
    def _(m):
        pl.semaphore_signal(barrier, inc=1, device_id=(flip_traced(ctx, m, n_ctx), ch), device_id_type=pl.DeviceIdType.MESH)

    ch_hops = [hop for hop in hops if hop[0] == "ch"]
    for hop in ch_hops:
        pl.semaphore_signal(barrier, inc=1, device_id=target(hop), device_id_type=pl.DeviceIdType.MESH)
    own_tok = pltpu.make_async_copy(tokens, tok.at[slot_of(0)], local_sems.at[0])
    own_tok.start()

    def w_columns(p, g):
        return w_send.at[:, :, pl.ds(pl.multiple_of(p * wide + g * LANES, LANES), LANES)]

    own_w = [pltpu.make_async_copy(w_columns(place, g), w_recv.at[g, 0], own_sems.at[0, g]) for g in range(lane_groups)]
    for copy in own_w:
        copy.start()
    own_lanes = pl.ds(pl.multiple_of(place * wide, LANES), wide)
    own_small = [
        pltpu.make_async_copy(all_taps.at[:, :, own_lanes], taps, local_sems.at[3]),
        pltpu.make_async_copy(all_gains.at[:, own_lanes], gains, local_sems.at[4]),
        pltpu.make_async_copy(all_decay.at[:, own_lanes], rates, local_sems.at[5]),
        pltpu.make_async_copy(all_skip.at[:, own_lanes], skip, local_sems.at[6]),
    ]
    for copy in own_small:
        copy.start()
    pl.semaphore_wait(barrier, n_ctx - 1 + len(ch_hops))

    def tok_copy(mask, i):
        src = tokens if mask == 0 else tok.at[slot_of(mask)]
        return pltpu.make_async_remote_copy(
            src_ref=src,
            dst_ref=tok.at[slot_of(mask)],
            send_sem=tok_ssem.at[mask, i],
            recv_sem=tok_rsem.at[mask | 1 << i],
            device_id=target(hops[i]),
            device_id_type=pl.DeviceIdType.MESH,
        )

    def arrived(mask):
        top = mask.bit_length() - 1
        pltpu.make_async_remote_copy(
            src_ref=tok.at[slot_of(mask)],
            dst_ref=tok.at[slot_of(mask)],
            send_sem=tok_ssem.at[0, top],
            recv_sem=tok_rsem.at[mask],
            device_id=target(hops[top]),
            device_id_type=pl.DeviceIdType.MESH,
        ).wait_recv()

    for i in range(depth):
        tok_copy(0, i).start()

    def w_copy(m, g):
        peer = flip_traced(ctx, m, n_ctx)
        return pltpu.make_async_remote_copy(
            src_ref=w_columns(peer % groups, g),
            dst_ref=w_recv.at[g, m],
            send_sem=w_ssem.at[g, m],
            recv_sem=w_rsem.at[g, m],
            device_id=(peer, ch),
            device_id_type=pl.DeviceIdType.MESH,
        )

    waiting = team < teams - 1

    def send(g, first, last):
        @pl.loop(first, last)
        def _(i):
            w_copy(2 * piece_order(i // 2, n_ctx // 2) + i % 2, g).start()

    for g in range(lane_groups - 1):
        send(g, 1, n_ctx)
    if lane_groups > 1:
        send(lane_groups - 1, 1, n_ctx - HELD)

        @pl.when(jnp.logical_not(waiting))
        def _():
            send(lane_groups - 1, n_ctx - HELD, n_ctx)
    else:
        send(0, 1, n_ctx)

    acc[...] = jnp.zeros_like(acc)
    masks = sorted(range(1, 2**depth), key=lambda m: (m.bit_length() if m.bit_length() == depth else 0, bin(m).count("1"), m))
    crossing = sum(1 << i for i in range(depth) if hops[i][0] == "ch")

    def gather(which):
        for mask in which:
            arrived(mask)
            for i in range(mask.bit_length(), depth):
                tok_copy(mask, i).start()

    gather([mask for mask in masks if not mask & crossing])
    own_tok.wait()
    for copy in own_w + own_small:
        copy.wait()
    rates[...] = rates[...] / (rows * n_ctx)

    header = SEGS

    modes = rates.shape[0]
    depth_rows = w_recv.shape[3]
    columns = [pl.ds(pl.multiple_of(place * wide + g * LANES, LANES), LANES) for g in range(lane_groups)]

    chips = n_ctx // 2
    per_half = chips // n_ch

    def near_first(i):
        home = ctx // 2
        origin = flip_traced(ch, i // per_half, n_ch) * per_half + flip_traced(home % per_half, i % per_half, per_half)
        return flip_traced(home, origin, chips)

    def in_order(i):
        return piece_order(i, chips)

    def project(g, first, last, source):
        @pl.loop(first, last)
        def _(i):
            m = 2 * source(i)
            odd = ctx % 2

            @pl.when(m > 0)
            def _():
                w_copy(m, g).wait_recv()

            w_copy(m + 1, g).wait_recv()
            origin = flip_traced(ctx - odd, m, n_ctx) * depth_rows
            half, column = origin // width, origin % width
            left = tok[pl.ds(half * groups, groups), :, pl.ds(pl.multiple_of(column, LANES), 2 * depth_rows)]
            left = left.reshape(span, 2 * depth_rows)
            pair = (m + odd, m + 1 - odd)
            right = jnp.concatenate(
                [jnp.concatenate([w_recv[g, p, j] for p in pair], axis=0) for j in range(3)], axis=1
            )
            acc[g, header:, :] += jnp.dot(left, right, preferred_element_type=jnp.float32)

    def halo_copy(g):
        return pltpu.make_async_remote_copy(
            src_ref=halo_out.at[g],
            dst_ref=halo.at[g],
            send_sem=halo_sems.at[g, 0],
            recv_sem=halo_sems.at[g, 1],
            device_id=((ctx + groups) % n_ctx, ch),
            device_id_type=pl.DeviceIdType.MESH,
        )

    def state_copy(k, g):
        return pltpu.make_async_remote_copy(
            src_ref=ends.at[g],
            dst_ref=carry.at[g, k],
            send_sem=st_ssem.at[g, k],
            recv_sem=st_rsem.at[g, k],
            device_id=((ctx + k * groups) % n_ctx, ch),
            device_id_type=pl.DeviceIdType.MESH,
        )

    def send_halo(g):
        halo_out[g] = acc[g, span : span + header, :]

        @pl.when(team < teams - 1)
        def _():
            halo_copy(g).start()

    def row(ref, m, mine):
        return jnp.broadcast_to(ref[m : m + 1, mine], (SEGS, LANES))

    def decays(mine):
        return [jnp.exp(-row(rates, m, mine)) for m in range(modes)]

    def first_half(g):
        mine = slice(g * LANES, (g + 1) * LANES)

        @pl.loop(1, SEGS + 1)
        def _(turn):
            s = turn % SEGS

            @pl.when(s == 0)
            def _():
                @pl.when(team == 0)
                def _():
                    acc[g, 0:header, :] = jnp.zeros((header, acc.shape[2]), jnp.float32)

                @pl.when(team > 0)
                def _():
                    halo_copy(g).wait_recv()
                    acc[g, 0:header, :] = halo[g]

            base = pl.multiple_of(s * seg, 8)
            features = []
            for j in range(3):
                block = acc[g, pl.ds(base, seg + header), j * LANES : (j + 1) * LANES]
                block = block.astype(jnp.bfloat16).astype(jnp.float32)
                total = taps[0, j : j + 1, mine] * block[header:]
                total += taps[1, j : j + 1, mine] * pltpu.roll(block, 1, 0)[header:]
                total += taps[2, j : j + 1, mine] * pltpu.roll(block, 2, 0)[header:]
                features.append(total)
            gate[g, pl.ds(s, seg, stride=SEGS), :] = features[0]
            prod[g, pl.ds(s, seg, stride=SEGS), :] = features[1] * features[2]

        keep = decays(mine)

        def first_step(t, states):
            x = prod[g, pl.ds(pl.multiple_of(t * SEGS, SEGS), SEGS), :]
            return tuple(a * s + x for a, s in zip(keep, states))

        zeros = tuple(jnp.zeros((SEGS, LANES), jnp.float32) for _ in range(modes))
        last = lax.fori_loop(0, seg, first_step, zeros, unroll=4)
        for m in range(modes):
            state[g, m] = last[m]

        rate = rates[:, mine]
        jump = jnp.exp(-rate * float(seg))
        running = jnp.zeros_like(jump)
        for s in range(SEGS):
            ending = state[g, :, s, :]
            state[g, :, s, :] = running
            running = running * jump + ending
        ends[g] = running
        carry[g, 0] = jnp.zeros_like(jump)
        for k in range(1, teams):
            @pl.when(team + k < teams)
            def _():
                state_copy(k, g).start()

    def second_half(g):
        mine = slice(g * LANES, (g + 1) * LANES)
        rate = rates[:, mine]
        for k in range(1, teams):
            @pl.when(team >= k)
            def _():
                state_copy(k, g).wait_recv()
                carry[g, 0] += carry[g, k] * jnp.exp(-rates[:, mine] * float((k - 1) * span))
        incoming = carry[g, 0]
        for s in range(SEGS):
            state[g, :, s, :] = state[g, :, s, :] + incoming * jnp.exp(-rate * float(s * seg))

        keep = decays(mine)
        weight = [row(gains, m, mine) * jnp.sqrt(2.0 * row(rates, m, mine)) for m in range(modes)]
        direct = jnp.broadcast_to(skip[0:1, mine], (SEGS, LANES))

        def second_step(t, states):
            where = pl.ds(pl.multiple_of(t * SEGS, SEGS), SEGS)
            x = prod[g, where, :]
            states = tuple(a * s + x for a, s in zip(keep, states))
            terms = [w * s for w, s in zip(weight, states)] + [direct * x]
            while len(terms) > 1:
                terms = [a + b for a, b in zip(terms[::2], terms[1::2])] + ([terms[-1]] if len(terms) % 2 else [])
            gate[g, where, :] = gate[g, where, :] * terms[0]
            return states

        lax.fori_loop(0, seg, second_step, tuple(state[g, m] for m in range(modes)), unroll=4)

        @pl.loop(0, SEGS)
        def _(s):
            value = gate[g, pl.ds(s, seg, stride=SEGS), :]
            sent[g, pl.ds(pl.multiple_of(s * seg, 8), seg), :] = value.astype(sent.dtype)

    def out_rows(p, g):
        return sent.at[g, pl.ds(pl.multiple_of(p * rows, 16), rows), :]

    def out_copy(d, g):
        peer = flip_traced(place, d, groups)
        return pltpu.make_async_remote_copy(
            src_ref=out_rows(peer, g),
            dst_ref=out.at[:, columns[g]],
            send_sem=out_ssem.at[g, d],
            recv_sem=out_rsem.at[g, d],
            device_id=(team * groups + peer, ch),
            device_id_type=pl.DeviceIdType.MESH,
        )

    def out_arrival(d, g):
        peer = flip_traced(place, d, groups)
        spot = out.at[:, pl.ds(pl.multiple_of(peer * wide + g * LANES, LANES), LANES)]
        return pltpu.make_async_remote_copy(
            src_ref=spot,
            dst_ref=spot,
            send_sem=out_ssem.at[g, d],
            recv_sem=out_rsem.at[g, d],
            device_id=(team * groups + peer, ch),
            device_id_type=pl.DeviceIdType.MESH,
        )

    own_out = [pltpu.make_async_copy(out_rows(place, g), out.at[:, columns[g]], own_sems.at[1, g]) for g in range(lane_groups)]
    def give_out(g):
        @pl.loop(1, groups)
        def _(d):
            out_copy(groups - d, g).start()

        own_out[g].start()

    tail = lane_groups - 1
    far = [mask for mask in masks if mask & crossing]
    if tail:
        project(0, 0, per_half, near_first)
    gather(far)
    for g in range(tail):
        project(g, per_half if g == 0 else 0, chips, near_first)
        send_halo(g)
        first_half(g)
        if g == tail - 1:
            @pl.when(waiting)
            def _():
                send(tail, n_ctx - HELD, n_ctx)

        if g < tail - 1:
            second_half(g)
            give_out(g)
    half_way = 0
    if tail:
        project(tail, 0, half_way, in_order)
        second_half(tail - 1)
        give_out(tail - 1)
        project(tail, half_way, chips, in_order)
    else:
        project(0, 0, chips, in_order)
    send_halo(tail)
    first_half(tail)
    second_half(tail)
    give_out(tail)

    for i in range(depth):
        tok_copy(0, i).wait_send()
    for mask in masks:
        for i in range(mask.bit_length(), depth):
            tok_copy(mask, i).wait_send()

    for g in range(lane_groups):
        @pl.loop(1, n_ctx)
        def _(m):
            w_copy(m, g).wait_send()

        @pl.when(team < teams - 1)
        def _():
            halo_copy(g).wait_send()

        for k in range(1, teams):
            @pl.when(team + k < teams)
            def _():
                state_copy(k, g).wait_send()

        @pl.loop(1, groups)
        def _(d):
            out_arrival(d, g).wait_recv()
            out_copy(d, g).wait_send()

        own_out[g].wait()


def body(n_ctx, n_ch, tokens, w_in, taps, modes_gain, decay, skip):
    rows, width = tokens.shape
    e_rows, _, channels = w_in.shape
    modes = decay.shape[0]
    groups = min(n_ctx // 2, channels // LANES)
    teams = n_ctx // groups
    wide = channels // groups
    span = groups * rows
    parts = wide // LANES
    depth = (groups * n_ch).bit_length() - 1
    w_send = w_in.transpose(1, 0, 2)
    hbm = pl.BlockSpec(memory_space=pl.ANY)
    dma = pltpu.SemaphoreType.DMA
    f32 = jnp.float32
    return pl.pallas_call(
        functools.partial(kernel, n_ctx, n_ch, groups),
        out_shape=jax.ShapeDtypeStruct((rows, channels), jnp.bfloat16),
        in_specs=[hbm] * 6,
        out_specs=hbm,
        scratch_shapes=[
            pltpu.VMEM((3, 3, wide), f32),
            pltpu.VMEM((modes, wide), f32),
            pltpu.VMEM((modes, wide), f32),
            pltpu.VMEM((1, wide), f32),
            pltpu.VMEM((n_ch * groups, rows, width), tokens.dtype),
            pltpu.VMEM((parts, n_ctx, 3, e_rows, LANES), w_in.dtype),
            pltpu.VMEM((parts, SEGS + span, 3 * LANES), f32),
            pltpu.VMEM((parts, span, LANES), f32),
            pltpu.VMEM((parts, span, LANES), f32),
            pltpu.VMEM((parts, modes, SEGS, LANES), f32),
            pltpu.VMEM((parts, modes, LANES), f32),
            pltpu.VMEM((parts, teams, modes, LANES), f32),
            pltpu.VMEM((parts, span, LANES), jnp.bfloat16),
            pltpu.VMEM((parts, SEGS, 3 * LANES), f32),
            pltpu.VMEM((parts, SEGS, 3 * LANES), f32),
            dma((2**depth, depth)),
            dma((2**depth,)),
            dma((parts, n_ctx)),
            dma((parts, n_ctx)),
            dma((parts, groups)),
            dma((parts, groups)),
            dma((parts, teams)),
            dma((parts, teams)),
            dma((parts, 2)),
            dma((7,)),
            dma((2, parts)),
        ],
        compiler_params=pltpu.CompilerParams(
            collective_id=0, has_side_effects=True, vmem_limit_bytes=60 * 1024 * 1024
        ),
    )(tokens, w_send, taps, modes_gain, decay, skip[None])


def solution(mesh):
    in_specs = (
        P("ctx", "ch"),
        P("ctx", None, "ch"),
        P(None, None, "ch"),
        P(None, "ch"),
        P(None, "ch"),
        P("ch"),
    )
    step = functools.partial(body, mesh.shape["ctx"], mesh.shape["ch"])
    return jax.shard_map(step, mesh=mesh, in_specs=in_specs, out_specs=P("ctx", "ch"), check_vma=False)
```

```python
import functools

import jax
import jax.numpy as jnp
from jax import lax
from jax.experimental import pallas as pl
from jax.experimental.pallas import tpu as pltpu
from jax.sharding import PartitionSpec as P

SEGS = 8
LANES = 128
HELD = 2
PARTS = 2


def flip(index, bits):
    out, bit = index, 1
    while bit <= bits:
        if bits & bit:
            out = out + bit - 2 * bit * ((index // bit) % 2)
        bit *= 2
    return out


def flip_traced(index, bits, count):
    out, bit = index, 1
    while bit < count:
        out = out + ((bits // bit) % 2) * (bit - 2 * bit * ((index // bit) % 2))
        bit *= 2
    return out


def piece_order(i, count):
    half = count // 2
    return jnp.where(i < half, 2 * i, 2 * (i - half) + 1)


def kernel(
    n_ctx, n_ch, groups,
    tokens, w_send, all_taps, all_gains, all_decay, all_skip, out,
    taps, gains, rates, skip, tok, w_recv, acc, prod, gate, state, ends, carry, sent, halo, halo_out,
    tok_ssem, tok_rsem, w_ssem, w_rsem, out_ssem, out_rsem, st_ssem, st_rsem, halo_sems, local_sems, own_sems,
):
    rows, width = tokens.shape
    wide = w_send.shape[2] // groups
    teams = n_ctx // groups
    span = groups * rows
    seg = span // SEGS
    lane_groups = wide // LANES
    ctx, ch = lax.axis_index("ctx"), lax.axis_index("ch")
    team, place = ctx // groups, ctx % groups

    hops = [("ctx", b) for b in reversed([2**i for i in range(1, groups.bit_length() - 1)])]
    hops += [("ch", b) for b in reversed([2**i for i in range(n_ch.bit_length() - 1)])]
    hops += [("ctx", 1)]
    depth = len(hops)

    def target(hop):
        axis, bit = hop
        return (flip(ctx, bit), ch) if axis == "ctx" else (ctx, flip(ch, bit))

    def slot_of(mask):
        cbits = sum(hops[i][1] for i in range(depth) if mask >> i & 1 and hops[i][0] == "ctx")
        hbits = sum(hops[i][1] for i in range(depth) if mask >> i & 1 and hops[i][0] == "ch")
        return flip(ch, hbits) * groups + flip(place, cbits)

    barrier = pltpu.get_barrier_semaphore()

    @pl.loop(1, n_ctx)
    def _(m):
        pl.semaphore_signal(barrier, inc=1, device_id=(flip_traced(ctx, m, n_ctx), ch), device_id_type=pl.DeviceIdType.MESH)

    ch_hops = [hop for hop in hops if hop[0] == "ch"]
    for hop in ch_hops:
        pl.semaphore_signal(barrier, inc=1, device_id=target(hop), device_id_type=pl.DeviceIdType.MESH)
    own_tok = pltpu.make_async_copy(tokens, tok.at[slot_of(0)], local_sems.at[0])
    own_tok.start()

    def w_columns(p, g):
        return w_send.at[:, :, pl.ds(pl.multiple_of(p * wide + g * LANES, LANES), LANES)]

    own_w = [pltpu.make_async_copy(w_columns(place, g), w_recv.at[g, 0], own_sems.at[0, g]) for g in range(lane_groups)]
    for copy in own_w:
        copy.start()
    own_lanes = pl.ds(pl.multiple_of(place * wide, LANES), wide)
    own_small = [
        pltpu.make_async_copy(all_taps.at[:, :, own_lanes], taps, local_sems.at[3]),
        pltpu.make_async_copy(all_gains.at[:, own_lanes], gains, local_sems.at[4]),
        pltpu.make_async_copy(all_decay.at[:, own_lanes], rates, local_sems.at[5]),
        pltpu.make_async_copy(all_skip.at[:, own_lanes], skip, local_sems.at[6]),
    ]
    for copy in own_small:
        copy.start()
    pl.semaphore_wait(barrier, n_ctx - 1 + len(ch_hops))

    def tok_copy(mask, i):
        src = tokens if mask == 0 else tok.at[slot_of(mask)]
        return pltpu.make_async_remote_copy(
            src_ref=src,
            dst_ref=tok.at[slot_of(mask)],
            send_sem=tok_ssem.at[mask, i],
            recv_sem=tok_rsem.at[mask | 1 << i],
            device_id=target(hops[i]),
            device_id_type=pl.DeviceIdType.MESH,
        )

    def arrived(mask):
        top = mask.bit_length() - 1
        pltpu.make_async_remote_copy(
            src_ref=tok.at[slot_of(mask)],
            dst_ref=tok.at[slot_of(mask)],
            send_sem=tok_ssem.at[0, top],
            recv_sem=tok_rsem.at[mask],
            device_id=target(hops[top]),
            device_id_type=pl.DeviceIdType.MESH,
        ).wait_recv()

    for i in range(depth):
        tok_copy(0, i).start()

    def w_copy(m, g):
        peer = flip_traced(ctx, m, n_ctx)
        return pltpu.make_async_remote_copy(
            src_ref=w_columns(peer % groups, g),
            dst_ref=w_recv.at[g, m],
            send_sem=w_ssem.at[g, m],
            recv_sem=w_rsem.at[g, m],
            device_id=(peer, ch),
            device_id_type=pl.DeviceIdType.MESH,
        )

    waiting = team < teams - 1

    def send(g, first, last):
        @pl.loop(first, last)
        def _(i):
            w_copy(2 * piece_order(i // 2, n_ctx // 2) + i % 2, g).start()

    for g in range(lane_groups - 1):
        send(g, 1, n_ctx)
    if lane_groups > 1:
        send(lane_groups - 1, 1, n_ctx - HELD)

        @pl.when(jnp.logical_not(waiting))
        def _():
            send(lane_groups - 1, n_ctx - HELD, n_ctx)
    else:
        send(0, 1, n_ctx)

    acc[...] = jnp.zeros_like(acc)
    masks = sorted(range(1, 2**depth), key=lambda m: (m.bit_length() if m.bit_length() == depth else 0, bin(m).count("1"), m))
    crossing = sum(1 << i for i in range(depth) if hops[i][0] == "ch")

    def gather(which):
        for mask in which:
            arrived(mask)
            for i in range(mask.bit_length(), depth):
                tok_copy(mask, i).start()

    gather([mask for mask in masks if not mask & crossing])
    own_tok.wait()
    for copy in own_w + own_small:
        copy.wait()
    rates[...] = rates[...] / (rows * n_ctx)

    header = SEGS
    piece = seg // PARTS
    whole = seg == rows

    modes = rates.shape[0]
    depth_rows = w_recv.shape[3]
    columns = [pl.ds(pl.multiple_of(place * wide + g * LANES, LANES), LANES) for g in range(lane_groups)]

    chips = n_ctx // 2
    per_half = chips // n_ch

    def near_first(i):
        home = ctx // 2
        origin = flip_traced(ch, i // per_half, n_ch) * per_half + flip_traced(home % per_half, i % per_half, per_half)
        return flip_traced(home, origin, chips)

    def in_order(i):
        return piece_order(i, chips)

    def project(g, first, last, source):
        @pl.loop(first, last)
        def _(i):
            m = 2 * source(i)
            odd = ctx % 2

            @pl.when(m > 0)
            def _():
                w_copy(m, g).wait_recv()

            w_copy(m + 1, g).wait_recv()
            origin = flip_traced(ctx - odd, m, n_ctx) * depth_rows
            half, column = origin // width, origin % width
            left = tok[pl.ds(half * groups, groups), :, pl.ds(pl.multiple_of(column, LANES), 2 * depth_rows)]
            left = left.reshape(span, 2 * depth_rows)
            pair = (m + odd, m + 1 - odd)
            right = jnp.concatenate(
                [jnp.concatenate([w_recv[g, p, j] for p in pair], axis=0) for j in range(3)], axis=1
            )
            acc[g, header:, :] += jnp.dot(left, right, preferred_element_type=jnp.float32)

    def halo_copy(g):
        return pltpu.make_async_remote_copy(
            src_ref=halo_out.at[g],
            dst_ref=halo.at[g],
            send_sem=halo_sems.at[g, 0],
            recv_sem=halo_sems.at[g, 1],
            device_id=((ctx + groups) % n_ctx, ch),
            device_id_type=pl.DeviceIdType.MESH,
        )

    def state_copy(k, g):
        return pltpu.make_async_remote_copy(
            src_ref=ends.at[g],
            dst_ref=carry.at[g, k],
            send_sem=st_ssem.at[g, k],
            recv_sem=st_rsem.at[g, k],
            device_id=((ctx + k * groups) % n_ctx, ch),
            device_id_type=pl.DeviceIdType.MESH,
        )

    def send_halo(g):
        halo_out[g] = acc[g, span : span + header, :]

        @pl.when(team < teams - 1)
        def _():
            halo_copy(g).start()

    def row(ref, m, mine):
        return jnp.broadcast_to(ref[m : m + 1, mine], (SEGS, LANES))

    def decays(mine):
        return [jnp.exp(-row(rates, m, mine)) for m in range(modes)]

    def first_half(g):
        mine = slice(g * LANES, (g + 1) * LANES)

        @pl.loop(1, SEGS + 1)
        def _(turn):
            s = turn % SEGS

            @pl.when(s == 0)
            def _():
                @pl.when(team == 0)
                def _():
                    acc[g, 0:header, :] = jnp.zeros((header, acc.shape[2]), jnp.float32)

                @pl.when(team > 0)
                def _():
                    halo_copy(g).wait_recv()
                    acc[g, 0:header, :] = halo[g]

            base = pl.multiple_of(s * seg, 8)
            features = []
            for j in range(3):
                block = acc[g, pl.ds(base, seg + header), j * LANES : (j + 1) * LANES]
                block = block.astype(jnp.bfloat16).astype(jnp.float32)
                total = taps[0, j : j + 1, mine] * block[header:]
                total += taps[1, j : j + 1, mine] * pltpu.roll(block, 1, 0)[header:]
                total += taps[2, j : j + 1, mine] * pltpu.roll(block, 2, 0)[header:]
                features.append(total)
            gate[g, pl.ds(s, seg, stride=SEGS), :] = features[0]
            prod[g, pl.ds(s, seg, stride=SEGS), :] = features[1] * features[2]

        keep = decays(mine)

        def first_step(t, states):
            x = prod[g, pl.ds(pl.multiple_of(t * SEGS, SEGS), SEGS), :]
            return tuple(a * s + x for a, s in zip(keep, states))

        zeros = tuple(jnp.zeros((SEGS, LANES), jnp.float32) for _ in range(modes))
        last = lax.fori_loop(0, seg, first_step, zeros, unroll=8)
        for m in range(modes):
            state[g, m] = last[m]

        rate = rates[:, mine]
        jump = jnp.exp(-rate * float(seg))
        running = jnp.zeros_like(jump)
        for s in range(SEGS):
            ending = state[g, :, s, :]
            state[g, :, s, :] = running
            running = running * jump + ending
        ends[g] = running
        carry[g, 0] = jnp.zeros_like(jump)
        for k in range(1, teams):
            @pl.when(team + k < teams)
            def _():
                state_copy(k, g).start()

    def second_half(g):
        mine = slice(g * LANES, (g + 1) * LANES)
        rate = rates[:, mine]
        for k in range(1, teams):
            @pl.when(team >= k)
            def _():
                state_copy(k, g).wait_recv()
                carry[g, 0] += carry[g, k] * jnp.exp(-rates[:, mine] * float((k - 1) * span))
        incoming = carry[g, 0]
        for s in range(SEGS):
            state[g, :, s, :] = state[g, :, s, :] + incoming * jnp.exp(-rate * float(s * seg))

        keep = decays(mine)
        weight = [row(gains, m, mine) * jnp.sqrt(2.0 * row(rates, m, mine)) for m in range(modes)]
        direct = jnp.broadcast_to(skip[0:1, mine], (SEGS, LANES))

        def second_step(t, states):
            where = pl.ds(pl.multiple_of(t * SEGS, SEGS), SEGS)
            x = prod[g, where, :]
            states = tuple(a * s + x for a, s in zip(keep, states))
            terms = [w * s for w, s in zip(weight, states)] + [direct * x]
            while len(terms) > 1:
                terms = [a + b for a, b in zip(terms[::2], terms[1::2])] + ([terms[-1]] if len(terms) % 2 else [])
            gate[g, where, :] = gate[g, where, :] * terms[0]
            return states

        states = tuple(state[g, m] for m in range(modes))
        for part in range(PARTS):
            states = lax.fori_loop(part * piece, (part + 1) * piece, second_step, states, unroll=8)

            @pl.loop(0, SEGS)
            def _(s):
                value = gate[g, pl.ds(part * piece * SEGS + s, piece, stride=SEGS), :]
                sent[g, pl.ds(pl.multiple_of(s * seg + part * piece, 16), piece), :] = value.astype(sent.dtype)

            if whole:
                give_out(g, part)
        if not whole:
            for part in range(PARTS):
                give_out(g, part)

    share = rows // PARTS

    def out_rows(p, g, part):
        return sent.at[g, pl.ds(pl.multiple_of(p * rows + part * share, 16), share), :]

    def out_copy(d, g, part):
        peer = flip_traced(place, d, groups)
        return pltpu.make_async_remote_copy(
            src_ref=out_rows(peer, g, part),
            dst_ref=out.at[part * share : (part + 1) * share, columns[g]],
            send_sem=out_ssem.at[g, part, d],
            recv_sem=out_rsem.at[g, part, d],
            device_id=(team * groups + peer, ch),
            device_id_type=pl.DeviceIdType.MESH,
        )

    def out_arrival(d, g, part):
        peer = flip_traced(place, d, groups)
        spot = out.at[part * share : (part + 1) * share, pl.ds(pl.multiple_of(peer * wide + g * LANES, LANES), LANES)]
        return pltpu.make_async_remote_copy(
            src_ref=spot,
            dst_ref=spot,
            send_sem=out_ssem.at[g, part, d],
            recv_sem=out_rsem.at[g, part, d],
            device_id=(team * groups + peer, ch),
            device_id_type=pl.DeviceIdType.MESH,
        )

    def own_out(g, part):
        return pltpu.make_async_copy(
            out_rows(place, g, part), out.at[part * share : (part + 1) * share, columns[g]], own_sems.at[1 + part, g]
        )

    def give_out(g, part):
        @pl.loop(1, groups)
        def _(d):
            out_copy(groups - d, g, part).start()

        own_out(g, part).start()

    tail = lane_groups - 1
    far = [mask for mask in masks if mask & crossing]
    if tail:
        project(0, 0, per_half, near_first)
    gather(far)
    for g in range(tail):
        project(g, per_half if g == 0 else 0, chips, near_first)
        send_halo(g)
        first_half(g)
        if g == tail - 1:
            @pl.when(waiting)
            def _():
                send(tail, n_ctx - HELD, n_ctx)

        if g < tail - 1:
            second_half(g)
    half_way = 0
    if tail:
        project(tail, 0, half_way, in_order)
        second_half(tail - 1)
        project(tail, half_way, chips, in_order)
    else:
        project(0, 0, chips, in_order)
    send_halo(tail)
    first_half(tail)
    second_half(tail)

    for i in range(depth):
        tok_copy(0, i).wait_send()
    for mask in masks:
        for i in range(mask.bit_length(), depth):
            tok_copy(mask, i).wait_send()

    for g in range(lane_groups):
        @pl.loop(1, n_ctx)
        def _(m):
            w_copy(m, g).wait_send()

        @pl.when(team < teams - 1)
        def _():
            halo_copy(g).wait_send()

        for k in range(1, teams):
            @pl.when(team + k < teams)
            def _():
                state_copy(k, g).wait_send()

        for part in range(PARTS):
            @pl.loop(1, groups)
            def _(d):
                out_arrival(d, g, part).wait_recv()
                out_copy(d, g, part).wait_send()

            own_out(g, part).wait()


def body(n_ctx, n_ch, tokens, w_in, taps, modes_gain, decay, skip):
    rows, width = tokens.shape
    e_rows, _, channels = w_in.shape
    modes = decay.shape[0]
    groups = min(n_ctx // 2, channels // LANES)
    teams = n_ctx // groups
    wide = channels // groups
    span = groups * rows
    parts = wide // LANES
    depth = (groups * n_ch).bit_length() - 1
    w_send = w_in.transpose(1, 0, 2)
    hbm = pl.BlockSpec(memory_space=pl.ANY)
    dma = pltpu.SemaphoreType.DMA
    f32 = jnp.float32
    return pl.pallas_call(
        functools.partial(kernel, n_ctx, n_ch, groups),
        out_shape=jax.ShapeDtypeStruct((rows, channels), jnp.bfloat16),
        in_specs=[hbm] * 6,
        out_specs=hbm,
        scratch_shapes=[
            pltpu.VMEM((3, 3, wide), f32),
            pltpu.VMEM((modes, wide), f32),
            pltpu.VMEM((modes, wide), f32),
            pltpu.VMEM((1, wide), f32),
            pltpu.VMEM((n_ch * groups, rows, width), tokens.dtype),
            pltpu.VMEM((parts, n_ctx, 3, e_rows, LANES), w_in.dtype),
            pltpu.VMEM((parts, SEGS + span, 3 * LANES), f32),
            pltpu.VMEM((parts, span, LANES), f32),
            pltpu.VMEM((parts, span, LANES), f32),
            pltpu.VMEM((parts, modes, SEGS, LANES), f32),
            pltpu.VMEM((parts, modes, LANES), f32),
            pltpu.VMEM((parts, teams, modes, LANES), f32),
            pltpu.VMEM((parts, span, LANES), jnp.bfloat16),
            pltpu.VMEM((parts, SEGS, 3 * LANES), f32),
            pltpu.VMEM((parts, SEGS, 3 * LANES), f32),
            dma((2**depth, depth)),
            dma((2**depth,)),
            dma((parts, n_ctx)),
            dma((parts, n_ctx)),
            dma((parts, PARTS, groups)),
            dma((parts, PARTS, groups)),
            dma((parts, teams)),
            dma((parts, teams)),
            dma((parts, 2)),
            dma((7,)),
            dma((1 + PARTS, parts)),
        ],
        compiler_params=pltpu.CompilerParams(
            collective_id=0, has_side_effects=True, vmem_limit_bytes=60 * 1024 * 1024
        ),
    )(tokens, w_send, taps, modes_gain, decay, skip[None])


def solution(mesh):
    in_specs = (
        P("ctx", "ch"),
        P("ctx", None, "ch"),
        P(None, None, "ch"),
        P(None, "ch"),
        P(None, "ch"),
        P("ch"),
    )
    step = functools.partial(body, mesh.shape["ctx"], mesh.shape["ch"])
    return jax.shard_map(step, mesh=mesh, in_specs=in_specs, out_specs=P("ctx", "ch"), check_vma=False)
```

```python
import functools

import jax
import jax.numpy as jnp
from jax import lax
from jax.experimental import pallas as pl
from jax.experimental.pallas import tpu as pltpu
from jax.sharding import PartitionSpec as P

SEGS = 8
LANES = 128
HELD = 2
PARTS = 2


def flip(index, bits):
    out, bit = index, 1
    while bit <= bits:
        if bits & bit:
            out = out + bit - 2 * bit * ((index // bit) % 2)
        bit *= 2
    return out


def flip_traced(index, bits, count):
    out, bit = index, 1
    while bit < count:
        out = out + ((bits // bit) % 2) * (bit - 2 * bit * ((index // bit) % 2))
        bit *= 2
    return out


def piece_order(i, count):
    half = count // 2
    return jnp.where(i < half, 2 * i, 2 * (i - half) + 1)


def kernel(
    n_ctx, n_ch, groups,
    tokens, w_send, all_taps, all_gains, all_decay, all_skip, out,
    taps, gains, rates, skip, tok, w_recv, acc, prod, gate, state, ends, carry, sent, halo, halo_out, coefs,
    tok_ssem, tok_rsem, w_ssem, w_rsem, out_ssem, out_rsem, st_ssem, st_rsem, halo_sems, local_sems, own_sems,
):
    rows, width = tokens.shape
    wide = w_send.shape[2] // groups
    teams = n_ctx // groups
    span = groups * rows
    seg = span // SEGS
    lane_groups = wide // LANES
    ctx, ch = lax.axis_index("ctx"), lax.axis_index("ch")
    team, place = ctx // groups, ctx % groups

    hops = [("ctx", b) for b in reversed([2**i for i in range(1, groups.bit_length() - 1)])]
    hops += [("ch", b) for b in reversed([2**i for i in range(n_ch.bit_length() - 1)])]
    hops += [("ctx", 1)]
    depth = len(hops)

    def target(hop):
        axis, bit = hop
        return (flip(ctx, bit), ch) if axis == "ctx" else (ctx, flip(ch, bit))

    def slot_of(mask):
        cbits = sum(hops[i][1] for i in range(depth) if mask >> i & 1 and hops[i][0] == "ctx")
        hbits = sum(hops[i][1] for i in range(depth) if mask >> i & 1 and hops[i][0] == "ch")
        return flip(ch, hbits) * groups + flip(place, cbits)

    barrier = pltpu.get_barrier_semaphore()

    @pl.loop(1, n_ctx)
    def _(m):
        pl.semaphore_signal(barrier, inc=1, device_id=(flip_traced(ctx, m, n_ctx), ch), device_id_type=pl.DeviceIdType.MESH)

    ch_hops = [hop for hop in hops if hop[0] == "ch"]
    for hop in ch_hops:
        pl.semaphore_signal(barrier, inc=1, device_id=target(hop), device_id_type=pl.DeviceIdType.MESH)
    own_tok = pltpu.make_async_copy(tokens, tok.at[slot_of(0)], local_sems.at[0])
    own_tok.start()

    def w_columns(p, g):
        return w_send.at[:, :, pl.ds(pl.multiple_of(p * wide + g * LANES, LANES), LANES)]

    own_w = [pltpu.make_async_copy(w_columns(place, g), w_recv.at[g, 0], own_sems.at[0, g]) for g in range(lane_groups)]
    for copy in own_w:
        copy.start()
    own_lanes = pl.ds(pl.multiple_of(place * wide, LANES), wide)
    own_small = [
        pltpu.make_async_copy(all_taps.at[:, :, own_lanes], taps, local_sems.at[3]),
        pltpu.make_async_copy(all_gains.at[:, own_lanes], gains, local_sems.at[4]),
        pltpu.make_async_copy(all_decay.at[:, own_lanes], rates, local_sems.at[5]),
        pltpu.make_async_copy(all_skip.at[:, own_lanes], skip, local_sems.at[6]),
    ]
    for copy in own_small:
        copy.start()
    pl.semaphore_wait(barrier, n_ctx - 1 + len(ch_hops))

    def tok_copy(mask, i):
        src = tokens if mask == 0 else tok.at[slot_of(mask)]
        return pltpu.make_async_remote_copy(
            src_ref=src,
            dst_ref=tok.at[slot_of(mask)],
            send_sem=tok_ssem.at[mask, i],
            recv_sem=tok_rsem.at[mask | 1 << i],
            device_id=target(hops[i]),
            device_id_type=pl.DeviceIdType.MESH,
        )

    def arrived(mask):
        top = mask.bit_length() - 1
        pltpu.make_async_remote_copy(
            src_ref=tok.at[slot_of(mask)],
            dst_ref=tok.at[slot_of(mask)],
            send_sem=tok_ssem.at[0, top],
            recv_sem=tok_rsem.at[mask],
            device_id=target(hops[top]),
            device_id_type=pl.DeviceIdType.MESH,
        ).wait_recv()

    for i in range(depth):
        tok_copy(0, i).start()

    def w_copy(m, g):
        peer = flip_traced(ctx, m, n_ctx)
        return pltpu.make_async_remote_copy(
            src_ref=w_columns(peer % groups, g),
            dst_ref=w_recv.at[g, m],
            send_sem=w_ssem.at[g, m],
            recv_sem=w_rsem.at[g, m],
            device_id=(peer, ch),
            device_id_type=pl.DeviceIdType.MESH,
        )

    waiting = team < teams - 1

    def send(g, first, last):
        @pl.loop(first, last)
        def _(i):
            w_copy(2 * piece_order(i // 2, n_ctx // 2) + i % 2, g).start()

    for g in range(lane_groups - 1):
        send(g, 1, n_ctx)
    if lane_groups > 1:
        send(lane_groups - 1, 1, n_ctx - HELD)

        @pl.when(jnp.logical_not(waiting))
        def _():
            send(lane_groups - 1, n_ctx - HELD, n_ctx)
    else:
        send(0, 1, n_ctx)

    acc[...] = jnp.zeros_like(acc)
    masks = sorted(range(1, 2**depth), key=lambda m: (m.bit_length() if m.bit_length() == depth else 0, bin(m).count("1"), m))
    crossing = sum(1 << i for i in range(depth) if hops[i][0] == "ch")

    def gather(which):
        for mask in which:
            arrived(mask)
            for i in range(mask.bit_length(), depth):
                tok_copy(mask, i).start()

    gather([mask for mask in masks if not mask & crossing])
    own_tok.wait()
    for copy in own_w + own_small:
        copy.wait()
    rates[...] = rates[...] / (rows * n_ctx)

    header = SEGS
    piece = seg // PARTS
    whole = seg == rows

    modes = rates.shape[0]
    depth_rows = w_recv.shape[3]
    columns = [pl.ds(pl.multiple_of(place * wide + g * LANES, LANES), LANES) for g in range(lane_groups)]

    chips = n_ctx // 2
    per_half = chips // n_ch

    def near_first(i):
        home = ctx // 2
        origin = flip_traced(ch, i // per_half, n_ch) * per_half + flip_traced(home % per_half, i % per_half, per_half)
        return flip_traced(home, origin, chips)

    def in_order(i):
        return piece_order(i, chips)

    def project(g, first, last, source):
        @pl.loop(first, last)
        def _(i):
            m = 2 * source(i)
            odd = ctx % 2

            @pl.when(m > 0)
            def _():
                w_copy(m, g).wait_recv()

            w_copy(m + 1, g).wait_recv()
            origin = flip_traced(ctx - odd, m, n_ctx) * depth_rows
            half, column = origin // width, origin % width
            left = tok[pl.ds(half * groups, groups), :, pl.ds(pl.multiple_of(column, LANES), 2 * depth_rows)]
            left = left.reshape(span, 2 * depth_rows)
            pair = (m + odd, m + 1 - odd)
            right = jnp.concatenate(
                [jnp.concatenate([w_recv[g, p, j] for p in pair], axis=0) for j in range(3)], axis=1
            )
            acc[g, header:, :] += jnp.dot(left, right, preferred_element_type=jnp.float32)

    def halo_copy(g):
        return pltpu.make_async_remote_copy(
            src_ref=halo_out.at[g],
            dst_ref=halo.at[g],
            send_sem=halo_sems.at[g, 0],
            recv_sem=halo_sems.at[g, 1],
            device_id=((ctx + groups) % n_ctx, ch),
            device_id_type=pl.DeviceIdType.MESH,
        )

    def state_copy(k, g):
        return pltpu.make_async_remote_copy(
            src_ref=ends.at[g],
            dst_ref=carry.at[g, k],
            send_sem=st_ssem.at[g, k],
            recv_sem=st_rsem.at[g, k],
            device_id=((ctx + k * groups) % n_ctx, ch),
            device_id_type=pl.DeviceIdType.MESH,
        )

    def send_halo(g):
        halo_out[g] = acc[g, span : span + header, :]

        @pl.when(team < teams - 1)
        def _():
            halo_copy(g).start()

    def row(ref, m, mine):
        return jnp.broadcast_to(ref[m : m + 1, mine], (SEGS, LANES))

    def prepare(g):
        mine = slice(g * LANES, (g + 1) * LANES)
        for m in range(modes):
            coefs[g, 0, m] = jnp.exp(-row(rates, m, mine))
            coefs[g, 1, m] = row(gains, m, mine) * jnp.sqrt(2.0 * row(rates, m, mine))

    def first_half(g):
        mine = slice(g * LANES, (g + 1) * LANES)

        @pl.loop(1, SEGS + 1)
        def _(turn):
            s = turn % SEGS

            @pl.when(s == 0)
            def _():
                @pl.when(team == 0)
                def _():
                    acc[g, 0:header, :] = jnp.zeros((header, acc.shape[2]), jnp.float32)

                @pl.when(team > 0)
                def _():
                    halo_copy(g).wait_recv()
                    acc[g, 0:header, :] = halo[g]

            base = pl.multiple_of(s * seg, 8)
            features = []
            for j in range(3):
                block = acc[g, pl.ds(base, seg + header), j * LANES : (j + 1) * LANES]
                block = block.astype(jnp.bfloat16).astype(jnp.float32)
                total = taps[0, j : j + 1, mine] * block[header:]
                total += taps[1, j : j + 1, mine] * pltpu.roll(block, 1, 0)[header:]
                total += taps[2, j : j + 1, mine] * pltpu.roll(block, 2, 0)[header:]
                features.append(total)
            gate[g, pl.ds(s, seg, stride=SEGS), :] = features[0]
            prod[g, pl.ds(s, seg, stride=SEGS), :] = features[1] * features[2]

        keep = [coefs[g, 0, m] for m in range(modes)]

        def first_step(t, states):
            x = prod[g, pl.ds(pl.multiple_of(t * SEGS, SEGS), SEGS), :]
            return tuple(a * s + x for a, s in zip(keep, states))

        zeros = tuple(jnp.zeros((SEGS, LANES), jnp.float32) for _ in range(modes))
        last = lax.fori_loop(0, seg, first_step, zeros, unroll=8)
        for m in range(modes):
            state[g, m] = last[m]

        rate = rates[:, mine]
        jump = jnp.exp(-rate * float(seg))
        running = jnp.zeros_like(jump)
        for s in range(SEGS):
            ending = state[g, :, s, :]
            state[g, :, s, :] = running
            running = running * jump + ending
        ends[g] = running
        carry[g, 0] = jnp.zeros_like(jump)
        for k in range(1, teams):
            @pl.when(team + k < teams)
            def _():
                state_copy(k, g).start()

    def second_half(g):
        mine = slice(g * LANES, (g + 1) * LANES)
        rate = rates[:, mine]
        for k in range(1, teams):
            @pl.when(team >= k)
            def _():
                state_copy(k, g).wait_recv()
                carry[g, 0] += carry[g, k] * jnp.exp(-rates[:, mine] * float((k - 1) * span))
        incoming = carry[g, 0]
        for s in range(SEGS):
            state[g, :, s, :] = state[g, :, s, :] + incoming * jnp.exp(-rate * float(s * seg))

        keep = [coefs[g, 0, m] for m in range(modes)]
        weight = [coefs[g, 1, m] for m in range(modes)]
        direct = jnp.broadcast_to(skip[0:1, mine], (SEGS, LANES))

        def second_step(t, states):
            where = pl.ds(pl.multiple_of(t * SEGS, SEGS), SEGS)
            x = prod[g, where, :]
            states = tuple(a * s + x for a, s in zip(keep, states))
            terms = [w * s for w, s in zip(weight, states)] + [direct * x]
            while len(terms) > 1:
                terms = [a + b for a, b in zip(terms[::2], terms[1::2])] + ([terms[-1]] if len(terms) % 2 else [])
            gate[g, where, :] = gate[g, where, :] * terms[0]
            return states

        states = tuple(state[g, m] for m in range(modes))
        for part in range(PARTS):
            states = lax.fori_loop(part * piece, (part + 1) * piece, second_step, states, unroll=8)

            @pl.loop(0, SEGS)
            def _(s):
                value = gate[g, pl.ds(part * piece * SEGS + s, piece, stride=SEGS), :]
                sent[g, pl.ds(pl.multiple_of(s * seg + part * piece, 16), piece), :] = value.astype(sent.dtype)

            if whole:
                give_out(g, part)
        if not whole:
            for part in range(PARTS):
                give_out(g, part)

    share = rows // PARTS

    def out_rows(p, g, part):
        return sent.at[g, pl.ds(pl.multiple_of(p * rows + part * share, 16), share), :]

    def out_copy(d, g, part):
        peer = flip_traced(place, d, groups)
        return pltpu.make_async_remote_copy(
            src_ref=out_rows(peer, g, part),
            dst_ref=out.at[part * share : (part + 1) * share, columns[g]],
            send_sem=out_ssem.at[g, part, d],
            recv_sem=out_rsem.at[g, part, d],
            device_id=(team * groups + peer, ch),
            device_id_type=pl.DeviceIdType.MESH,
        )

    def out_arrival(d, g, part):
        peer = flip_traced(place, d, groups)
        spot = out.at[part * share : (part + 1) * share, pl.ds(pl.multiple_of(peer * wide + g * LANES, LANES), LANES)]
        return pltpu.make_async_remote_copy(
            src_ref=spot,
            dst_ref=spot,
            send_sem=out_ssem.at[g, part, d],
            recv_sem=out_rsem.at[g, part, d],
            device_id=(team * groups + peer, ch),
            device_id_type=pl.DeviceIdType.MESH,
        )

    def own_out(g, part):
        return pltpu.make_async_copy(
            out_rows(place, g, part), out.at[part * share : (part + 1) * share, columns[g]], own_sems.at[1 + part, g]
        )

    def give_out(g, part):
        @pl.loop(1, groups)
        def _(d):
            out_copy(groups - d, g, part).start()

        own_out(g, part).start()

    tail = lane_groups - 1
    for g in range(lane_groups):
        prepare(g)
    far = [mask for mask in masks if mask & crossing]
    if tail:
        project(0, 0, per_half, near_first)
    gather(far)
    for g in range(tail):
        project(g, per_half if g == 0 else 0, chips, near_first)
        send_halo(g)
        first_half(g)
        if g == tail - 1:
            @pl.when(waiting)
            def _():
                send(tail, n_ctx - HELD, n_ctx)

        if g < tail - 1:
            second_half(g)
    half_way = 0
    if tail:
        project(tail, 0, half_way, in_order)
        second_half(tail - 1)
        project(tail, half_way, chips, in_order)
    else:
        project(0, 0, chips, in_order)
    send_halo(tail)
    first_half(tail)
    second_half(tail)

    for i in range(depth):
        tok_copy(0, i).wait_send()
    for mask in masks:
        for i in range(mask.bit_length(), depth):
            tok_copy(mask, i).wait_send()

    for g in range(lane_groups):
        @pl.loop(1, n_ctx)
        def _(m):
            w_copy(m, g).wait_send()

        @pl.when(team < teams - 1)
        def _():
            halo_copy(g).wait_send()

        for k in range(1, teams):
            @pl.when(team + k < teams)
            def _():
                state_copy(k, g).wait_send()

        for part in range(PARTS):
            @pl.loop(1, groups)
            def _(d):
                out_arrival(d, g, part).wait_recv()
                out_copy(d, g, part).wait_send()

            own_out(g, part).wait()


def body(n_ctx, n_ch, tokens, w_in, taps, modes_gain, decay, skip):
    rows, width = tokens.shape
    e_rows, _, channels = w_in.shape
    modes = decay.shape[0]
    groups = min(n_ctx // 2, channels // LANES)
    teams = n_ctx // groups
    wide = channels // groups
    span = groups * rows
    parts = wide // LANES
    depth = (groups * n_ch).bit_length() - 1
    w_send = w_in.transpose(1, 0, 2)
    hbm = pl.BlockSpec(memory_space=pl.ANY)
    dma = pltpu.SemaphoreType.DMA
    f32 = jnp.float32
    return pl.pallas_call(
        functools.partial(kernel, n_ctx, n_ch, groups),
        out_shape=jax.ShapeDtypeStruct((rows, channels), jnp.bfloat16),
        in_specs=[hbm] * 6,
        out_specs=hbm,
        scratch_shapes=[
            pltpu.VMEM((3, 3, wide), f32),
            pltpu.VMEM((modes, wide), f32),
            pltpu.VMEM((modes, wide), f32),
            pltpu.VMEM((1, wide), f32),
            pltpu.VMEM((n_ch * groups, rows, width), tokens.dtype),
            pltpu.VMEM((parts, n_ctx, 3, e_rows, LANES), w_in.dtype),
            pltpu.VMEM((parts, SEGS + span, 3 * LANES), f32),
            pltpu.VMEM((parts, span, LANES), f32),
            pltpu.VMEM((parts, span, LANES), f32),
            pltpu.VMEM((parts, modes, SEGS, LANES), f32),
            pltpu.VMEM((parts, modes, LANES), f32),
            pltpu.VMEM((parts, teams, modes, LANES), f32),
            pltpu.VMEM((parts, span, LANES), jnp.bfloat16),
            pltpu.VMEM((parts, SEGS, 3 * LANES), f32),
            pltpu.VMEM((parts, SEGS, 3 * LANES), f32),
            pltpu.VMEM((parts, 2, modes, SEGS, LANES), f32),
            dma((2**depth, depth)),
            dma((2**depth,)),
            dma((parts, n_ctx)),
            dma((parts, n_ctx)),
            dma((parts, PARTS, groups)),
            dma((parts, PARTS, groups)),
            dma((parts, teams)),
            dma((parts, teams)),
            dma((parts, 2)),
            dma((7,)),
            dma((1 + PARTS, parts)),
        ],
        compiler_params=pltpu.CompilerParams(
            collective_id=0, has_side_effects=True, vmem_limit_bytes=60 * 1024 * 1024
        ),
    )(tokens, w_send, taps, modes_gain, decay, skip[None])


def solution(mesh):
    in_specs = (
        P("ctx", "ch"),
        P("ctx", None, "ch"),
        P(None, None, "ch"),
        P(None, "ch"),
        P(None, "ch"),
        P("ch"),
    )
    step = functools.partial(body, mesh.shape["ctx"], mesh.shape["ch"])
    return jax.shard_map(step, mesh=mesh, in_specs=in_specs, out_specs=P("ctx", "ch"), check_vma=False)
```
